32 devices in a mesh: trade: 8 (over y, x, core), path: 4 (over z).
Axes of the slice: x: 2, y: 2, z: 4, core: 2. Of those that a mesh axis runs over, the one named last changes fastest.
Arguments:
- deltas: bfloat16 [32768, 512], P('trade', 'path'), may hold values from -0.0039978027 to 0.0039978027
- net_ids: int32 [32768], P('trade'), may hold values from 0 to 7, as said below
- block_ids: int32 [32768], P('trade'), may hold values from 0 to 13823
- bucket_map: int32 [13824], replicated, may hold values from 0 to 1151
- risk_weight: float32 [13824], replicated, may hold values from 10 to 80
- counts: int32 [8], P('trade'), may hold values from 1 to 4096, 19660 in all
- correlation: float32 [1152, 1152], replicated, may hold values from -1 to 3, as said below
- path_weight: float32 [512], P('path'), may hold values from 0.2 to 16.2, as said below
- margin_cotangent: float32 [8, 512], P(None, 'path'), may hold values from -6 to 6
Outputs:
- margin: float32 [8, 512], P(None, 'path')
- expected: float32 [8], replicated
- trade_grad: bfloat16 [32768, 512], P('trade', 'path')
The draws below stay inside these ranges and needn't reach their ends.
Inputs may be any that keep to these rules, and one draw needn't show every extreme that they name: The live trades of group g fill its first counts[g] of 4096 slots; some group is full. `net_ids`: among the 4096 slots of one trade group each netting set appears at most 768 times, and in every group one netting set appears exactly 768 times. `correlation`: symmetric and positive definite. `path_weight`: Positive.
All inputs are finite; a program needn't handle non-finite values.
Results may differ from the reference program's by a relative error of at most 0.0054.
The reference program's roundings to bfloat16 on the way (of `weighted` and `bucket_grad`) count: a program that leaves them out, or rounds other values in their place, can miss the bound.
Values may be sent and summed in bfloat16 or wider, within the bound.
No kernel may reach another device: no remote copies, remote signals or barrier semaphores. Data moves between devices by JAX's collectives and lax.ppermute only.
A program may use at most 64 MiB of HBM per device.

```python
import math
import jax
import jax.numpy as jnp
import numpy as np
from jax import lax

BUCKETS = 1152
TENOR_BLOCKS = 13824
NETS = 8
TRADE_CAP = 4096
MOST = 768
GROUPS = 8
TRADES = 32768
PATHS = 512
N_TRADE = 8


def draw_net_ids(key, part):
    group_total = TRADES // TRADE_CAP
    pool_size = NETS * MOST
    pool = (jnp.arange(pool_size, dtype=jnp.int32) // MOST).astype(jnp.int32)
    base_key = jax.random.fold_in(key, 31)

    def one_group(group):
        group_key = jax.random.fold_in(base_key, group)
        first_key = jax.random.fold_in(group_key, 1)
        second_key = jax.random.fold_in(group_key, 2)
        third_key = jax.random.fold_in(group_key, 3)
        special = jax.random.randint(first_key, (), 0, NETS, dtype=jnp.int32)
        order = jax.random.permutation(second_key, pool_size).astype(jnp.int32)
        score = jnp.where(pool == special, order - pool_size, order).astype(jnp.int32)
        picked = pool[jnp.argsort(score, stable=True)[:TRADE_CAP]]
        shuffle = jax.random.permutation(third_key, TRADE_CAP).astype(jnp.int32)
        return picked[shuffle]
    return lax.map(one_group, jnp.arange(group_total, dtype=jnp.int32)).reshape(TRADES).astype(jnp.int32)


def draw_correlation(key, part):
    factor_key = jax.random.fold_in(key, 11)
    factor = jax.random.normal(factor_key, (BUCKETS, BUCKETS), jnp.float32)
    product = jnp.dot(factor, factor.T, precision=lax.Precision.HIGHEST) / BUCKETS
    return 0.5 * (product + product.T) + 0.5 * jnp.eye(BUCKETS, dtype=jnp.float32)


def draw_path_weight(key, part):
    jitter_key = jax.random.fold_in(key, 23)
    position = jnp.arange(PATHS, dtype=jnp.float32) / max(PATHS - 1, 1)
    rising = 1.0 + 2.0 * position
    jitter = jax.random.uniform(jitter_key, (PATHS,), jnp.float32, 0.5, 1.5)
    return rising * jitter


def set_ends(entries, key, smallest, largest):
    shape = entries.shape
    spot = [jax.random.randint(jax.random.fold_in(key, axis), (), 0, shape[axis]) for axis in range(len(shape))]
    entries = entries.at[tuple(spot)].set(smallest)
    longest = shape.index(max(shape))
    spot[longest] = (spot[longest] + 1) % shape[longest]
    return entries.at[tuple(spot)].set(largest)


def block_levels(rng, shape, cuts, low, largest):
    loudness, own = 1.0, jax.random.fold_in(rng, 6)
    for dim, shards_of in cuts:
        heights = jnp.exp(jax.random.uniform(jax.random.fold_in(own, dim), (shards_of,), jnp.float32, low / len(cuts), largest / len(cuts)))
        loudness = loudness * jnp.repeat(heights, shape[dim] // shards_of).reshape([-1 if axis == dim else 1 for axis in range(len(shape))])
    return loudness


def split_up(amount, total, most, slope):
    portions = [(1 << 20) // math.isqrt(grade ** slope) + 1 for grade in range(2, amount + 1)]
    rest, given = total - most - (amount - 1), [1] * (amount - 1)
    while rest > 0:
        candidates = [i for i in range(amount - 1) if given[i] < most]
        whole, left = sum([portions[i] for i in candidates]), rest
        for i in candidates:
            extra = min(most - given[i], max(1, left * portions[i] // whole), rest)
            given[i] = given[i] + extra
            rest = rest - extra
    return np.array([most] + given)


def ragged_sizes(stream_key, amount, total, reach, lean):
    if amount == 2:
        one = jax.random.randint(stream_key, (), max(1, total - reach), min(reach, total - 1) + 1)
        return jnp.stack([one, total - one])
    sizes = jnp.asarray(split_up(amount, total, reach, lean), jnp.int32)
    couples = (amount - 1) // 2
    source_of, receiver = sizes[1:1 + 2 * couples:2], sizes[2:2 + 2 * couples:2]
    slack = jnp.minimum(source_of - 1, reach - receiver)
    shifted = jax.random.randint(jax.random.fold_in(stream_key, 1), (couples,), 0, 1 << 20) % (slack + 1)
    sizes = sizes.at[1:1 + 2 * couples:2].set(source_of - shifted).at[2:2 + 2 * couples:2].set(receiver + shifted)
    return sizes[jax.random.permutation(jax.random.fold_in(stream_key, 2), amount)]


def centred(rng, shape, spread, most, cuts=(), kind=jnp.bfloat16):
    loudness = block_levels(rng, shape, cuts, -0.22, 0.18) if cuts else 1.0
    values = jax.random.normal(rng, shape, jnp.float32) * spread * loudness
    return jnp.minimum(jnp.maximum(values, -most), most).astype(kind)


def setup_inputs(seed: int = 0) -> dict:
    arg_keys = jax.random.split(jax.random.key(seed), 10)
    return {
        "deltas": centred(arg_keys[0], (TRADES, PATHS), 0.0005, 0.0039978027, ((0, 8), (1, 4))),
        "net_ids": draw_net_ids(jax.random.fold_in(arg_keys[9], 71), 0),
        "block_ids": set_ends(jax.random.randint(arg_keys[2], (TRADES,), 0, TENOR_BLOCKS), jax.random.fold_in(arg_keys[2], 1), 0, TENOR_BLOCKS - 1).astype(jnp.int32),
        "bucket_map": set_ends(jax.random.randint(arg_keys[3], (TENOR_BLOCKS,), 0, BUCKETS), jax.random.fold_in(arg_keys[3], 1), 0, BUCKETS - 1).astype(jnp.int32),
        "risk_weight": jnp.clip(jnp.exp(jax.random.uniform(arg_keys[4], (TENOR_BLOCKS,), jnp.float32, math.log(10.0), math.log(80.0))), 10.0, 80.0),
        "counts": ragged_sizes(arg_keys[5], GROUPS, TRADE_CAP * N_TRADE * 3 // 5, TRADE_CAP, 2).astype(jnp.int32),
        "correlation": draw_correlation(jax.random.fold_in(arg_keys[9], 71), 0),
        "path_weight": draw_path_weight(jax.random.fold_in(arg_keys[9], 71), 0),
        "margin_cotangent": centred(arg_keys[8], (NETS, PATHS), 1.0, 6.0, ((1, 4),), jnp.float32),
    }


EPSILON = 1e-06

def reference(deltas, net_ids, block_ids, bucket_map, risk_weight, counts, correlation, path_weight, margin_cotangent):
    total_slots = deltas.shape[0]
    path_total = deltas.shape[1]
    position = jnp.arange(total_slots, dtype=jnp.int32)
    group_of = (position // TRADE_CAP).astype(jnp.int32)
    slot_of = (position % TRADE_CAP).astype(jnp.int32)
    is_live = slot_of < counts[group_of]
    trade_weight = risk_weight[block_ids]
    trade_bucket = bucket_map[block_ids]
    weighted = jnp.where(is_live[:, None], trade_weight[:, None] * deltas.astype(jnp.float32), 0.0).astype(jnp.bfloat16)
    segment_key = (trade_bucket * NETS + net_ids).astype(jnp.int32)
    summed = jax.ops.segment_sum(weighted.astype(jnp.float32), segment_key, num_segments=BUCKETS * NETS)
    summed = summed.reshape(BUCKETS, NETS * path_total)
    coupled = jnp.dot(correlation, summed, precision=lax.Precision.HIGHEST, preferred_element_type=jnp.float32)
    quad_form = lax.optimization_barrier(jnp.sum(summed * coupled, axis=0))
    margin_flat = jnp.sqrt(quad_form + EPSILON)
    margin = margin_flat.reshape(NETS, path_total)
    expected = lax.optimization_barrier(jnp.sum(margin * path_weight[None, :], axis=1)) / PATHS
    bucket_grad = ((margin_cotangent.reshape(NETS * path_total) / margin_flat)[None, :] * coupled).astype(jnp.bfloat16)
    bucket_grad = bucket_grad.reshape(BUCKETS, NETS, path_total)
    chosen = bucket_grad[trade_bucket, net_ids]
    trade_grad = jnp.where(is_live[:, None], trade_weight[:, None] * chosen.astype(jnp.float32), 0.0).astype(jnp.bfloat16)
    return (margin, expected, trade_grad)
```

```python
import functools

import jax
import jax.numpy as jnp
from jax import lax
from jax.experimental import pallas as pl
from jax.experimental.pallas import tpu as pltpu
from jax.sharding import PartitionSpec as P

EPSILON = 1e-06
LANES = 128
SUPER = 8
DEAD = 255
KEY_SPLIT = 4


F32 = jnp.float32
BF16 = jnp.bfloat16
I32 = jnp.int32


def bf16_pieces(value, number):
    pieces = []
    rest = value
    for _ in range(number):
        piece = rest.astype(BF16)
        pieces.append(piece)
        rest = rest - piece.astype(F32)
    return pieces


def prep_kernel(
    groups,
    width,
    padded,
    half,
    picks,
    me_ref,
    count_ref,
    ids_ref,
    nets_ref,
    rw_ref,
    bm_ref,
    deltas_ref,
    *rest,
):
    outs = rest[:groups]
    w_ref, b_scr, sliced = rest[groups:]
    rows = ids_ref.shape[0]
    table_rows = rw_ref.shape[0]
    hi_count = -(-table_rows // LANES) * LANES
    rw = rw_ref[...]
    bm = bm_ref[...]
    if hi_count > table_rows:
        spare = hi_count - table_rows
        rw = jnp.concatenate([rw, jnp.zeros((spare, LANES), F32)], 0)
        bm = jnp.concatenate([bm, jnp.zeros((spare, LANES), I32)], 0)
    b_low = (bm & 7).astype(F32)
    b_high = (bm - (bm & 7)).astype(F32)
    w_table = jnp.concatenate(bf16_pieces(rw.T, 3), 1)
    b_table = jnp.concatenate([b_high.T.astype(BF16), b_low.T.astype(BF16)], 1)
    hi_iota = lax.broadcasted_iota(I32, (hi_count, 2 * LANES), 0)
    lo_iota = lax.broadcasted_iota(I32, (LANES, 2 * LANES), 0)

    def find(pair, carry):
        first = ids_ref[pl.ds(2 * pair, 1), :]
        second = ids_ref[pl.ds(2 * pair + 1, 1), :]
        both = jnp.concatenate([first, second], 1)
        hot = jnp.where(hi_iota == both // LANES, F32(1), F32(0)).astype(BF16)
        w_all = jnp.dot(
            w_table, jnp.concatenate([hot, hot, hot], 0), preferred_element_type=F32
        )
        b_all = jnp.dot(b_table, jnp.concatenate([hot, hot], 0), preferred_element_type=F32)
        low = lo_iota == both % LANES
        w_row = jnp.sum(jnp.where(low, w_all, 0.0), axis=0, keepdims=True)
        b_row = jnp.sum(jnp.where(low, b_all, 0.0), axis=0, keepdims=True)
        w_ref[pl.ds(2 * pair, 1), :] = w_row[:, :LANES]
        w_ref[pl.ds(2 * pair + 1, 1), :] = w_row[:, LANES:]
        b_scr[pl.ds(2 * pair, 1), :] = b_row[:, :LANES]
        b_scr[pl.ds(2 * pair + 1, 1), :] = b_row[:, LANES:]
        return carry

    lax.fori_loop(0, rows // 2, find, 0, unroll=4)
    place = lax.broadcasted_iota(I32, (rows, LANES), 0) * LANES + lax.broadcasted_iota(
        I32, (rows, LANES), 1
    )
    live = place < count_ref[0]
    w_ref[...] = jnp.where(live, w_ref[...], 0.0)
    bucket = b_scr[...].astype(I32)
    upper = (bucket >= half).astype(I32)
    inside = bucket - half * upper
    key_a = jnp.where(live, inside // KEY_SPLIT, DEAD).astype(F32)
    key_b = (inside % KEY_SPLIT * picks + upper * (picks // 2) + nets_ref[...]).astype(F32)
    base = rows * padded
    for number in range(rows // SUPER):
        cut = slice(number * SUPER, (number + 1) * SUPER)
        tile = jnp.concatenate([key_a[cut], key_b[cut]], 0).astype(BF16)
        for out in outs:
            out[base + 2 * SUPER * number : base + 2 * SUPER * (number + 1), :] = tile

    def turn(row, carry):
        block = deltas_ref[pl.ds(pl.multiple_of(row * LANES, LANES), LANES), :]
        turned = block.astype(F32).T * w_ref[pl.ds(row, 1), :]
        for dest in range(groups):
            piece = turned[dest * width : (dest + 1) * width]
            if padded > width:
                piece = jnp.concatenate([piece, jnp.zeros((padded - width, LANES), F32)], 0)
            sliced[row, dest] = piece.astype(BF16)
        return carry

    lax.fori_loop(0, rows, turn, 0, unroll=4)

    def place_out(row, carry):
        start = pl.multiple_of(row * padded, padded)
        for step in range(groups):
            outs[step][pl.ds(start, padded), :] = sliced[row, me_ref[0] ^ step]
        return carry

    lax.fori_loop(0, rows, place_out, 0, unroll=4)


def decode_keys(read, rows, picks, hi_scr, sel_scr):
    total = jnp.zeros((SUPER, LANES), F32)
    for number in range(rows // SUPER):
        tile = read(2 * SUPER * number).astype(F32)
        key_a = tile[:SUPER]
        key_b = tile[SUPER:].astype(I32)
        cut = slice(number * SUPER, (number + 1) * SUPER)
        hi_scr[cut, :] = key_a.astype(I32) * KEY_SPLIT + key_b // picks
        sel_scr[cut, :] = key_b % picks
        total = total + jnp.where(key_a < DEAD, F32(1), F32(0))
    count = jnp.sum(total).astype(I32)
    span = SUPER * LANES
    return (count + span - 1) // span


def hot_block(hi_scr, number, half):
    iota = lax.broadcasted_iota(I32, (half, LANES), 0)
    parts = []
    for step in range(SUPER):
        row = hi_scr[pl.ds(number * SUPER + step, 1), :]
        parts.append(jnp.where(iota == row, F32(1), F32(0)).astype(BF16))
    return jnp.concatenate(parts, 1)


def scatter_kernel(number_of, has_start, rows, padded, half, picks, *refs):
    chunks = refs[:number_of]
    rest = refs[number_of:]
    if has_start:
        start_ref, out, hi_scr, sel_scr = rest
        out[...] = start_ref[...]
    else:
        out, hi_scr, sel_scr = rest
        out[...] = jnp.zeros_like(out)
    base = rows * padded
    for chunk in chunks:
        blocks = decode_keys(
            lambda at, chunk=chunk: chunk[base + at : base + at + 2 * SUPER, :],
            rows,
            picks,
            hi_scr,
            sel_scr,
        )

        def add(number, carry, chunk=chunk):
            hot = hot_block(hi_scr, number, half)
            parts = []
            for step in range(SUPER):
                at = pl.multiple_of((number * SUPER + step) * padded, padded)
                values = chunk[pl.ds(at, padded), :].astype(F32)
                select = sel_scr[pl.ds(number * SUPER + step, 1), :]
                parts.append(
                    jnp.concatenate(
                        [
                            jnp.where(select == pick, values, 0.0).astype(BF16)
                            for pick in range(picks)
                        ],
                        0,
                    )
                )
            spread = jnp.concatenate(parts, 1)
            out[...] += lax.dot_general(
                hot, spread, (((1,), (1,)), ((), ())), preferred_element_type=F32
            )
            return carry

        lax.fori_loop(0, blocks, add, 0)


def middle_kernel(
    half, step_rows, cot_ref, table_ref, corr_ref, grad_ref, margin_ref, sums, parts, coup, quad
):
    step = pl.program_id(0)
    buckets = sums.shape[0]
    across = sums.shape[1]

    @pl.when(step == 0)
    def _():
        sums[:half, :] = table_ref[:, :across]
        sums[half:, :] = table_ref[: buckets - half, across:]
        high, low = bf16_pieces(sums[...], 2)
        parts[:, :across] = high
        parts[:, across:] = low
        quad[...] = jnp.zeros_like(quad)

    at = pl.multiple_of(step * step_rows, step_rows)
    high, low = bf16_pieces(corr_ref[...], 2)
    pair = jnp.dot(high, parts[...], preferred_element_type=F32)
    other = jnp.dot(low, parts[...], preferred_element_type=F32)
    coupled = (pair[:, :across] + pair[:, across:]) + (other[:, :across] + other[:, across:])
    coup[pl.ds(at, step_rows), :] = coupled
    quad[...] += jnp.sum(coupled * sums[pl.ds(at, step_rows), :], axis=0, keepdims=True)

    @pl.when(step == pl.num_programs(0) - 1)
    def _():
        margin = jnp.sqrt(quad[...] + EPSILON)
        ratio = cot_ref[...] / margin
        turned = (ratio * coup[...]).T.astype(BF16)
        grad_ref[:across, :] = turned[:, :half]
        grad_ref[across:, : buckets - half] = turned[:, half:]
        if 2 * half > buckets:
            grad_ref[across:, buckets - half :] = jnp.zeros((across, 2 * half - buckets), BF16)
        tail = jnp.concatenate(
            [piece.astype(F32) for piece in bf16_pieces(margin, 3)]
            + [jnp.zeros((2 * SUPER - 3, across), F32)],
            0,
        )
        margin_ref[...] = tail.astype(BF16)


def lookup_kernel(rows, padded, half, picks, grad_ref, tail_ref, keys_ref, out, hi_scr, sel_scr):
    blocks = decode_keys(
        lambda at: keys_ref[at : at + 2 * SUPER, :], rows, picks, hi_scr, sel_scr
    )
    base = rows * padded
    out[base:, :] = tail_ref[...]

    def look(number, carry):
        hot = hot_block(hi_scr, number, half)
        found = jnp.dot(grad_ref[...], hot, preferred_element_type=F32)
        for step in range(SUPER):
            select = sel_scr[pl.ds(number * SUPER + step, 1), :]
            total = jnp.zeros((padded, LANES), F32)
            for pick in range(picks):
                part = found[pick * padded : (pick + 1) * padded, step * LANES : (step + 1) * LANES]
                total = total + jnp.where(select == pick, part, 0.0)
            at = pl.multiple_of((number * SUPER + step) * padded, padded)
            out[pl.ds(at, padded), :] = total.astype(BF16)
        return carry

    lax.fori_loop(0, blocks, look, 0)

    def clear(number, carry):
        span = SUPER * padded
        at = pl.multiple_of(number * span, span)
        out[pl.ds(at, span), :] = jnp.zeros((span, LANES), BF16)
        return carry

    lax.fori_loop(blocks, rows // SUPER, clear, 0)


def unpack_kernel(groups, width, padded, me_ref, count_ref, w_ref, *rest):
    chunks = rest[:groups]
    out, margin_ref, gathered, sem = rest[groups:]
    rows = w_ref.shape[0]
    copies = []
    for step in range(groups):
        copy = pltpu.make_async_copy(
            chunks[step], gathered.at[me_ref[0] ^ step], sem.at[step]
        )
        copy.start()
        copies.append(copy)
    for copy in copies:
        copy.wait()
    base = rows * padded
    for dest in range(groups):
        tail = gathered[dest, base:, :].astype(F32)
        margin_ref[dest : dest + 1, :] = (tail[0:1] + tail[1:2]) + tail[2:3]

    def turn(row, carry):
        at = pl.multiple_of(row * padded, padded)
        parts = [gathered[dest, pl.ds(at, padded), :].astype(F32)[:width] for dest in range(groups)]
        place = row * LANES + lax.broadcasted_iota(I32, (1, LANES), 1)
        scaled = jnp.where(
            place < count_ref[0], w_ref[pl.ds(row, 1), :] * jnp.concatenate(parts, 0), 0.0
        )
        out[pl.ds(pl.multiple_of(row * LANES, LANES), LANES), :] = scaled.T.astype(BF16)
        return carry

    lax.fori_loop(0, rows, turn, 0, unroll=4)


def shards(
    deltas,
    net_ids,
    block_ids,
    bucket_map,
    risk_weight,
    counts,
    correlation,
    path_weight,
    margin_cotangent,
):
    capacity, path_count = deltas.shape
    buckets = correlation.shape[0]
    nets = margin_cotangent.shape[0]
    groups = lax.axis_size("trade")
    slabs = lax.axis_size("path")
    width = path_count // groups
    padded = max(width, 2 * SUPER)
    rows = capacity // LANES
    picks = 2 * nets
    across = nets * padded
    half = -(-buckets // (2 * LANES)) * LANES
    chunk_rows = rows * padded + 2 * rows
    back_rows = rows * padded + 2 * SUPER
    me = lax.axis_index("trade")
    me_one = me.astype(I32).reshape(1)
    table_len = -(-risk_weight.shape[0] // LANES) * LANES
    spare = table_len - risk_weight.shape[0]
    rw = jnp.pad(risk_weight, (0, spare)).reshape(-1, LANES)
    bm = jnp.pad(bucket_map, (0, spare)).reshape(-1, LANES)
    ids = block_ids.reshape(rows, LANES)
    nets_rows = net_ids.reshape(rows, LANES)

    vmem = pl.BlockSpec(memory_space=pltpu.VMEM)
    smem = pl.BlockSpec(memory_space=pltpu.SMEM)

    *outgoing, weight = pl.pallas_call(
        functools.partial(prep_kernel, groups, width, padded, half, picks),
        out_shape=[jax.ShapeDtypeStruct((chunk_rows, LANES), BF16)] * groups
        + [jax.ShapeDtypeStruct((rows, LANES), F32)],
        in_specs=[smem, smem] + [vmem] * 5,
        out_specs=[vmem] * (groups + 1),
        scratch_shapes=[
            pltpu.VMEM((rows, LANES), F32),
            pltpu.VMEM((rows, groups, padded, LANES), BF16),
        ],
        name="prep",
    )(me_one, counts, ids, nets_rows, rw, bm, deltas)

    def swap(value, step):
        return lax.ppermute(value, "trade", [(i, i ^ step) for i in range(groups)])

    arrived = [outgoing[0]] + [swap(outgoing[step], step) for step in range(1, groups)]

    key_scratch = [pltpu.VMEM((rows, LANES), I32), pltpu.VMEM((rows, LANES), I32)]

    def scatter(chunks, start):
        operands = list(chunks) + ([] if start is None else [start])
        return pl.pallas_call(
            functools.partial(
                scatter_kernel, len(chunks), start is not None, rows, padded, half, picks
            ),
            out_shape=jax.ShapeDtypeStruct((half, 2 * across), F32),
            in_specs=[vmem] * len(operands),
            out_specs=vmem,
            scratch_shapes=key_scratch,
            name="scatter",
        )(*operands)

    table = None
    for first in range(0, groups, 2):
        table = scatter(arrived[first : first + 2], table)

    def own_row(value):
        own = lax.dynamic_slice_in_dim(value, me * width, width, value.ndim - 1)
        return jnp.pad(own, ((0, 0), (0, padded - width))).reshape(1, across)

    cot_row = own_row(margin_cotangent)
    step_rows = LANES
    grad, tail = pl.pallas_call(
        functools.partial(middle_kernel, half, step_rows),
        grid=(buckets // step_rows,),
        out_shape=[
            jax.ShapeDtypeStruct((2 * across, half), BF16),
            jax.ShapeDtypeStruct((2 * SUPER, across), BF16),
        ],
        in_specs=[
            pl.BlockSpec((1, across), lambda i: (0, 0)),
            pl.BlockSpec((half, 2 * across), lambda i: (0, 0)),
            pl.BlockSpec((step_rows, buckets), lambda i: (i, 0)),
        ],
        out_specs=[
            pl.BlockSpec((2 * across, half), lambda i: (0, 0)),
            pl.BlockSpec((2 * SUPER, across), lambda i: (0, 0)),
        ],
        scratch_shapes=[
            pltpu.VMEM((buckets, across), F32),
            pltpu.VMEM((buckets, 2 * across), BF16),
            pltpu.VMEM((buckets, across), F32),
            pltpu.VMEM((1, across), F32),
        ],
        name="middle",
    )(cot_row, table, correlation)

    key_rows = 2 * rows
    key_at = rows * padded // key_rows

    def lookup(chunk):
        return pl.pallas_call(
            functools.partial(lookup_kernel, rows, padded, half, picks),
            grid=(1,),
            out_shape=jax.ShapeDtypeStruct((back_rows, LANES), BF16),
            in_specs=[
                pl.BlockSpec((2 * across, half), lambda i: (0, 0)),
                pl.BlockSpec((2 * SUPER, across), lambda i: (0, 0)),
                pl.BlockSpec((key_rows, LANES), lambda i: (key_at, 0)),
            ],
            out_specs=pl.BlockSpec((back_rows, LANES), lambda i: (0, 0)),
            scratch_shapes=key_scratch,
            name="lookup",
        )(grad, tail, chunk)

    returned = [None] * groups
    for step in list(range(groups - 1, 0, -1)) + [0]:
        answer = lookup(arrived[step])
        returned[step] = swap(answer, step) if step else answer

    trade_grad, margins = pl.pallas_call(
        functools.partial(unpack_kernel, groups, width, padded),
        out_shape=[
            jax.ShapeDtypeStruct((capacity, path_count), BF16),
            jax.ShapeDtypeStruct((groups, across), F32),
        ],
        in_specs=[smem, smem, vmem] + [pl.BlockSpec(memory_space=pl.ANY)] * groups,
        out_specs=[vmem, vmem],
        scratch_shapes=[
            pltpu.VMEM((groups, back_rows, LANES), BF16),
            pltpu.SemaphoreType.DMA((groups,)),
        ],
        name="unpack",
    )(me_one, counts, weight, *returned)

    margin = (
        margins.reshape(groups, nets, padded)[:, :, :width]
        .transpose(1, 0, 2)
        .reshape(nets, path_count)
    )
    partial = jnp.sum(margin * path_weight[None, :], axis=1)
    expected = lax.psum(partial, "path") / (path_count * slabs)
    return (margin, expected, trade_grad)


def solution(mesh):
    placed = (
        P("trade", "path"),
        P("trade"),
        P("trade"),
        P(),
        P(),
        P("trade"),
        P(),
        P("path"),
        P(None, "path"),
    )
    return jax.shard_map(
        shards,
        mesh=mesh,
        in_specs=placed,
        out_specs=(P(None, "path"), P(), P("trade", "path")),
        check_vma=False,
    )
```

```python
import functools

import jax
import jax.numpy as jnp
from jax import lax
from jax.experimental import pallas as pl
from jax.experimental.pallas import tpu as pltpu
from jax.sharding import PartitionSpec as P

EPSILON = 1e-06
LANES = 128
SUPER = 8
DEAD = 255
KEY_SPLIT = 4
VMEM_LIMIT = 16 * 1024 * 1024
WIDE_LIMIT = 60 * 1024 * 1024
EARLY = 2


F32 = jnp.float32
BF16 = jnp.bfloat16
I32 = jnp.int32


def params(limit=VMEM_LIMIT):
    return pltpu.CompilerParams(vmem_limit_bytes=limit)


def steps_of(groups):
    def turned(bits):
        return bits & ~6 | (bits & 2) << 1 | (bits & 4) >> 1

    if groups < 8:
        return [(bits, bits) for bits in range(groups)]
    near = [0, 1, 2, 4, 3, 5]
    order = near + [bits for bits in range(groups) if bits not in near]
    return [(bits, turned(bits)) for bits in order]


def peer(me, step):
    even, odd = step
    if even == odd:
        return me ^ even
    return me ^ jnp.where(me % 2 == 1, odd, even)


def bf16_pieces(value, number):
    pieces = []
    rest = value
    for _ in range(number):
        piece = rest.astype(BF16)
        pieces.append(piece)
        rest = rest - piece.astype(F32)
    return pieces


def prep_kernel(
    groups,
    width,
    padded,
    half,
    picks,
    me_ref,
    count_ref,
    *rest,
):
    sources = rest[:5]
    outs = rest[5 : 5 + groups]
    w_ref, b_scr, sliced, *locals_, sem = rest[5 + groups :]
    ids_ref, nets_ref, rw_ref, bm_ref, deltas_ref = locals_
    copies = [
        pltpu.make_async_copy(source, local, sem.at[number])
        for number, (source, local) in enumerate(zip(sources, locals_))
    ]
    for copy in copies:
        copy.start()
    for copy in copies[:4]:
        copy.wait()
    rows = ids_ref.shape[0]
    table_rows = rw_ref.shape[0]
    hi_count = -(-table_rows // LANES) * LANES
    rw = rw_ref[...]
    bm = bm_ref[...]
    if hi_count > table_rows:
        spare = hi_count - table_rows
        rw = jnp.concatenate([rw, jnp.zeros((spare, LANES), F32)], 0)
        bm = jnp.concatenate([bm, jnp.zeros((spare, LANES), I32)], 0)
    b_low = (bm & 7).astype(F32)
    b_high = (bm - (bm & 7)).astype(F32)
    w_table = jnp.concatenate(bf16_pieces(rw.T, 3), 1)
    b_table = jnp.concatenate([b_high.T.astype(BF16), b_low.T.astype(BF16)], 1)
    hi_iota = lax.broadcasted_iota(I32, (hi_count, 2 * LANES), 0)
    lo_iota = lax.broadcasted_iota(I32, (LANES, 2 * LANES), 0)

    def find(pair, carry):
        first = ids_ref[pl.ds(2 * pair, 1), :]
        second = ids_ref[pl.ds(2 * pair + 1, 1), :]
        both = jnp.concatenate([first, second], 1)
        hot = jnp.where(hi_iota == both // LANES, F32(1), F32(0)).astype(BF16)
        w_all = jnp.dot(
            w_table, jnp.concatenate([hot, hot, hot], 0), preferred_element_type=F32
        )
        b_all = jnp.dot(b_table, jnp.concatenate([hot, hot], 0), preferred_element_type=F32)
        low = lo_iota == both % LANES
        w_row = jnp.sum(jnp.where(low, w_all, 0.0), axis=0, keepdims=True)
        b_row = jnp.sum(jnp.where(low, b_all, 0.0), axis=0, keepdims=True)
        w_ref[pl.ds(2 * pair, 1), :] = w_row[:, :LANES]
        w_ref[pl.ds(2 * pair + 1, 1), :] = w_row[:, LANES:]
        b_scr[pl.ds(2 * pair, 1), :] = b_row[:, :LANES]
        b_scr[pl.ds(2 * pair + 1, 1), :] = b_row[:, LANES:]
        return carry

    lax.fori_loop(0, rows // 2, find, 0, unroll=4)
    place = lax.broadcasted_iota(I32, (rows, LANES), 0) * LANES + lax.broadcasted_iota(
        I32, (rows, LANES), 1
    )
    live = place < count_ref[0]
    w_ref[...] = jnp.where(live, w_ref[...], 0.0)
    bucket = b_scr[...].astype(I32)
    upper = (bucket >= half).astype(I32)
    inside = bucket - half * upper
    key_a = jnp.where(live, inside // KEY_SPLIT, DEAD).astype(F32)
    key_b = (inside % KEY_SPLIT * picks + upper * (picks // 2) + nets_ref[...]).astype(F32)
    base = rows * padded
    for number in range(rows // SUPER):
        cut = slice(number * SUPER, (number + 1) * SUPER)
        tile = jnp.concatenate([key_a[cut], key_b[cut]], 0).astype(BF16)
        for out in outs:
            out[base + 2 * SUPER * number : base + 2 * SUPER * (number + 1), :] = tile

    copies[4].wait()

    def turn(row, carry):
        block = deltas_ref[pl.ds(pl.multiple_of(row * LANES, LANES), LANES), :]
        turned = block.astype(F32).T * w_ref[pl.ds(row, 1), :]
        for dest in range(groups):
            piece = turned[dest * width : (dest + 1) * width]
            if padded > width:
                piece = jnp.concatenate([piece, jnp.zeros((padded - width, LANES), F32)], 0)
            sliced[row, dest] = piece.astype(BF16)
        return carry

    lax.fori_loop(0, rows, turn, 0, unroll=4)

    peers = [peer(me_ref[0], step) for step in steps_of(groups)]

    def place_out(row, carry):
        start = pl.multiple_of(row * padded, padded)
        for number in range(groups):
            outs[number][pl.ds(start, padded), :] = sliced[row, peers[number]]
        return carry

    lax.fori_loop(0, rows, place_out, 0, unroll=4)


def decode_keys(read, rows, picks, half, split, hi_scr, sel_scr):
    nets = picks // 2
    parts = -(-2 * half // split)
    total = jnp.zeros((SUPER, LANES), F32)
    for number in range(rows // SUPER):
        tile = read(2 * SUPER * number).astype(F32)
        key_a = tile[:SUPER]
        key_b = tile[SUPER:].astype(I32)
        cut = slice(number * SUPER, (number + 1) * SUPER)
        place = key_a.astype(I32) * KEY_SPLIT + key_b // picks
        select = key_b % picks
        if split != half:
            upper = select // nets
            place = place + upper * half
            select = select - upper * nets
            part = jnp.zeros_like(place)
            for number_of in range(1, parts):
                part = part + jnp.where(place >= number_of * split, 1, 0)
            place = jnp.where(key_a < DEAD, place - part * split, split)
            select = select + part * nets
        hi_scr[cut, :] = place
        sel_scr[cut, :] = select
        total = total + jnp.where(key_a < DEAD, F32(1), F32(0))
    count = jnp.sum(total).astype(I32)
    span = SUPER * LANES
    return (count + span - 1) // span


def scatter_kernel(number_of, has_start, rows, padded, half, picks, *refs):
    chunks = refs[:number_of]
    rest = refs[number_of:]
    if has_start:
        start_ref, out, hi_scr, sel_scr = rest
        out[...] = start_ref[...]
    else:
        out, hi_scr, sel_scr = rest
        out[...] = jnp.zeros_like(out)
    base = rows * padded
    for chunk in chunks:
        blocks = decode_keys(
            lambda at, chunk=chunk: chunk[base + at : base + at + 2 * SUPER, :],
            rows,
            picks,
            half,
            half,
            hi_scr,
            sel_scr,
        )

        def add(number, wide, chunk=chunk):
            iota = lax.broadcasted_iota(I32, (half, LANES), 0)
            hot, spread = [], []
            for step in range(wide * SUPER):
                row = number * SUPER + step
                hot.append(
                    jnp.where(iota == hi_scr[pl.ds(row, 1), :], F32(1), F32(0)).astype(BF16)
                )
                at = pl.multiple_of(row * padded, padded)
                values = chunk[pl.ds(at, padded), :].astype(F32)
                select = sel_scr[pl.ds(row, 1), :]
                spread.append(
                    jnp.concatenate(
                        [
                            jnp.where(select == pick, values, 0.0).astype(BF16)
                            for pick in range(picks)
                        ],
                        0,
                    )
                )
            out[...] += lax.dot_general(
                jnp.concatenate(hot, 1),
                jnp.concatenate(spread, 1),
                (((1,), (1,)), ((), ())),
                preferred_element_type=F32,
            )

        @pl.loop(0, blocks // 2)
        def _(number):
            add(2 * number, 2)

        @pl.when(blocks % 2 == 1)
        def _():
            add(blocks - 1, 1)


def middle_kernel(
    half,
    step_rows,
    width,
    me_ref,
    cot_ref,
    weight_ref,
    table_ref,
    corr_ref,
    grad_ref,
    margin_ref,
    share_ref,
    *scratch,
):
    sums, parts, coup = scratch
    buckets, across = sums.shape
    nets = cot_ref.shape[0]
    padded = across // nets
    lane = lax.broadcasted_iota(I32, (1, across), 1)
    turn = lax.rem(across - me_ref[0] * width, across)
    cot = pltpu.roll(cot_ref[...], turn, 1)
    weight = pltpu.roll(jnp.broadcast_to(weight_ref[...], (nets, across)), turn, 1)
    cot_row = jnp.zeros((1, across), F32)
    weight_row = jnp.zeros((1, across), F32)
    for net in range(nets):
        inside = (lane >= net * padded) & (lane < net * padded + width)
        shift = net * padded
        own = cot[net : net + 1]
        share = weight[:1]
        if shift:
            own = pltpu.roll(own, shift, 1)
            share = pltpu.roll(share, shift, 1)
        cot_row = jnp.where(inside, own, cot_row)
        weight_row = jnp.where(inside, share, weight_row)
    sums[:half, :] = table_ref[:, :across]
    sums[half:, :] = table_ref[: buckets - half, across:]
    high, low = bf16_pieces(sums[...], 2)
    parts[:, :across] = high
    parts[:, across:] = low

    def couple(step, quad):
        at = pl.multiple_of(step * step_rows, step_rows)
        high, low = bf16_pieces(corr_ref[pl.ds(at, step_rows), :], 2)
        pair = jnp.dot(high, parts[...], preferred_element_type=F32)
        other = jnp.dot(low, parts[...], preferred_element_type=F32)
        coupled = (pair[:, :across] + pair[:, across:]) + (other[:, :across] + other[:, across:])
        coup[pl.ds(at, step_rows), :] = coupled
        return quad + jnp.sum(coupled * sums[pl.ds(at, step_rows), :], axis=0, keepdims=True)

    quad = lax.fori_loop(0, buckets // step_rows, couple, jnp.zeros((1, across), F32))
    margin = jnp.sqrt(quad + EPSILON)
    ratio = cot_row / margin
    split = grad_ref.shape[1]
    for part in range(grad_ref.shape[0] // across):
        first, last = part * split, min((part + 1) * split, buckets)
        piece = ratio * coup[first:last, :]
        if last - first < split:
            piece = jnp.concatenate(
                [piece, jnp.zeros((split - (last - first), across), F32)], 0
            )
        grad_ref[part * across : (part + 1) * across, :] = piece.T.astype(BF16)
    margin_ref[...] = jnp.broadcast_to(margin, (SUPER, across))
    share_ref[...] = jnp.broadcast_to(margin * weight_row, (SUPER, across))


def tail_kernel(slabs, answers, slab_ref, margin_ref, *refs):
    shares = refs[:slabs]
    out, *filled, share_scr, sem = refs[slabs + answers :]
    for step, share in enumerate(shares):
        share_scr[slab_ref[0] ^ step] = share[...]
    total = share_scr[0]
    for step in range(1, len(shares)):
        total = total + share_scr[step]
    pieces = [
        piece.astype(F32)[:1]
        for value in (margin_ref[...], total)
        for piece in bf16_pieces(value, 3)
    ]
    blank = jnp.zeros((2 * SUPER - len(pieces), LANES), F32)
    out[...] = jnp.concatenate(pieces + [blank], 0).astype(BF16)
    copies = []
    for number, answer in enumerate(filled):
        base = answer.shape[0] - 2 * SUPER
        copy = pltpu.make_async_copy(
            out, answer.at[pl.ds(base, 2 * SUPER), :], sem.at[number]
        )
        copy.start()
        copies.append(copy)
    for copy in copies:
        copy.wait()


def lookup_kernel(rows, padded, half, split, picks, has_tail, keys_ref, grad_ref, *refs):
    out, hi_scr, sel_scr = refs[-3:]
    base = rows * padded
    blocks = decode_keys(
        lambda at: keys_ref[base + at : base + at + 2 * SUPER, :],
        rows,
        picks,
        half,
        split,
        hi_scr,
        sel_scr,
    )
    if has_tail:
        out[base:, :] = refs[0][...]
    iota = lax.broadcasted_iota(I32, (split, LANES), 0)
    choices = grad_ref.shape[0] // padded

    def look(number, carry):
        for pair in range(SUPER // 2):
            first = number * SUPER + 2 * pair
            hot = jnp.concatenate(
                [
                    jnp.where(iota == hi_scr[pl.ds(first + i, 1), :], F32(1), F32(0)).astype(BF16)
                    for i in range(2)
                ],
                1,
            )
            found = jnp.dot(grad_ref[...], hot, preferred_element_type=F32)
            for i in range(2):
                select = sel_scr[pl.ds(first + i, 1), :]
                total = jnp.zeros((padded, LANES), F32)
                for pick in range(choices):
                    part = found[pick * padded : (pick + 1) * padded, i * LANES : (i + 1) * LANES]
                    total = jnp.where(select == pick, part, total)
                at = pl.multiple_of((first + i) * padded, padded)
                out[pl.ds(at, padded), :] = total.astype(BF16)
        return carry

    lax.fori_loop(0, blocks, look, 0)

    def clear(number, carry):
        span = SUPER * padded
        at = pl.multiple_of(number * span, span)
        out[pl.ds(at, span), :] = jnp.zeros((span, LANES), BF16)
        return carry

    lax.fori_loop(blocks, rows // SUPER, clear, 0)


def unpack_kernel(groups, width, padded, paths, me_ref, count_ref, w_ref, *rest):
    chunks = rest[:groups]
    tail_ref, out, margin_ref, expected_ref, gathered = rest[groups:]
    rows = w_ref.shape[0]
    base = rows * padded
    nets = margin_ref.shape[0]
    gathered[me_ref[0], :base, :] = chunks[0][:base, :]
    gathered[me_ref[0], base:, :] = tail_ref[...]
    for number, step in enumerate(steps_of(groups)[1:], 1):
        gathered[peer(me_ref[0], step)] = chunks[number][...]
    total = jnp.zeros((1, LANES), F32)
    for dest in range(groups):
        tail = gathered[dest, base:, :].astype(F32)
        own = (tail[0:1] + tail[1:2]) + tail[2:3]
        total = total + ((tail[3:4] + tail[4:5]) + tail[5:6])
        for net in range(nets):
            margin_ref[net : net + 1, dest * width : (dest + 1) * width] = own[
                :, net * padded : net * padded + width
            ]
    group = lax.broadcasted_iota(I32, (1, LANES), 1) // padded
    for net in range(nets):
        expected_ref[net] = jnp.sum(jnp.where(group == net, total, 0.0)) / paths

    def turn(row, carry):
        at = pl.multiple_of(row * padded, padded)
        parts = [gathered[dest, pl.ds(at, padded), :].astype(F32)[:width] for dest in range(groups)]
        place = row * LANES + lax.broadcasted_iota(I32, (1, LANES), 1)
        scaled = jnp.where(
            place < count_ref[0], w_ref[pl.ds(row, 1), :] * jnp.concatenate(parts, 0), 0.0
        )
        out[pl.ds(pl.multiple_of(row * LANES, LANES), LANES), :] = scaled.T.astype(BF16)
        return carry

    lax.fori_loop(0, rows, turn, 0, unroll=4)


def shards(
    deltas,
    net_ids,
    block_ids,
    bucket_map,
    risk_weight,
    counts,
    correlation,
    path_weight,
    margin_cotangent,
):
    capacity, path_count = deltas.shape
    buckets = correlation.shape[0]
    nets = margin_cotangent.shape[0]
    groups = lax.axis_size("trade")
    slabs = lax.axis_size("path")
    width = path_count // groups
    padded = max(width, 2 * SUPER)
    rows = capacity // LANES
    picks = 2 * nets
    across = nets * padded
    half = -(-buckets // (4 * SUPER)) * 2 * SUPER
    parts = -(-buckets // 256)
    split = -(-buckets // (parts * 2 * SUPER)) * 2 * SUPER
    chunk_rows = rows * padded + 2 * rows
    back_rows = rows * padded + 2 * SUPER
    me = lax.axis_index("trade")
    me_one = me.astype(I32).reshape(1)
    table_len = -(-risk_weight.shape[0] // LANES) * LANES
    spare = table_len - risk_weight.shape[0]
    rw = jnp.pad(risk_weight, (0, spare)).reshape(-1, LANES)
    bm = jnp.pad(bucket_map, (0, spare)).reshape(-1, LANES)
    ids = block_ids.reshape(rows, LANES)
    nets_rows = net_ids.reshape(rows, LANES)

    vmem = pl.BlockSpec(memory_space=pltpu.VMEM)
    smem = pl.BlockSpec(memory_space=pltpu.SMEM)

    *outgoing, weight = pl.pallas_call(
        functools.partial(prep_kernel, groups, width, padded, half, picks),
        out_shape=[jax.ShapeDtypeStruct((chunk_rows, LANES), BF16)] * groups
        + [jax.ShapeDtypeStruct((rows, LANES), F32)],
        in_specs=[smem, smem] + [pl.BlockSpec(memory_space=pltpu.HBM)] * 5,
        out_specs=[vmem] * (groups + 1),
        scratch_shapes=[
            pltpu.VMEM((rows, LANES), F32),
            pltpu.VMEM((rows, groups, padded, LANES), BF16),
        ]
        + [pltpu.VMEM(value.shape, value.dtype) for value in (ids, nets_rows, rw, bm, deltas)]
        + [pltpu.SemaphoreType.DMA((5,))],
        name="prep",
        compiler_params=params(WIDE_LIMIT),
    )(me_one, counts, ids, nets_rows, rw, bm, deltas)

    steps = steps_of(groups)

    def send(value, number):
        pairs = [(i, i ^ steps[number][i % 2]) for i in range(groups)]
        return lax.ppermute(value, "trade", pairs)

    def send_back(value, number):
        pairs = [(i ^ steps[number][i % 2], i) for i in range(groups)]
        return lax.ppermute(value, "trade", pairs)

    key_scratch = [pltpu.VMEM((rows, LANES), I32), pltpu.VMEM((rows, LANES), I32)]

    def scatter(chunks, start):
        operands = list(chunks) + ([] if start is None else [start])
        return pl.pallas_call(
            functools.partial(
                scatter_kernel, len(chunks), start is not None, rows, padded, half, picks
            ),
            out_shape=jax.ShapeDtypeStruct((half, 2 * across), F32),
            in_specs=[vmem] * len(operands),
            out_specs=vmem,
            scratch_shapes=key_scratch,
            name="scatter",
        compiler_params=params(),
        )(*operands)

    near = groups // 2 + groups // 4
    arrived = [outgoing[0]] + [send(outgoing[step], step) for step in range(1, near)]
    table = scatter(arrived[:2], None)
    *late, table = lax.optimization_barrier((*outgoing[near:], table))
    arrived += [send(value, near + step) for step, value in enumerate(late)]
    for first in range(2, near, 2):
        table = scatter(arrived[first : first + 2], table)
    for step in range(near, groups):
        table = scatter(arrived[step : step + 1], table)

    grad, margins, share = pl.pallas_call(
        functools.partial(middle_kernel, half, LANES, width),
        out_shape=[
            jax.ShapeDtypeStruct((parts * across, split), BF16),
            jax.ShapeDtypeStruct((SUPER, across), F32),
            jax.ShapeDtypeStruct((SUPER, across), F32),
        ],
        in_specs=[smem] + [vmem] * 4,
        out_specs=[vmem] * 3,
        scratch_shapes=[
            pltpu.VMEM((buckets, across), F32),
            pltpu.VMEM((buckets, 2 * across), BF16),
            pltpu.VMEM((buckets, across), F32),
        ],
        name="middle",
        compiler_params=params(),
    )(me_one, margin_cotangent, path_weight.reshape(1, path_count), table, correlation)

    shares = [share] + [
        lax.ppermute(share, "path", [(i, i ^ step) for i in range(slabs)])
        for step in range(1, slabs)
    ]
    slab_one = lax.axis_index("path").astype(I32).reshape(1)
    def lookup(chunk, extra):
        return pl.pallas_call(
            functools.partial(lookup_kernel, rows, padded, half, split, picks, bool(extra)),
            out_shape=jax.ShapeDtypeStruct((back_rows, LANES), BF16),
            in_specs=[vmem] * (2 + len(extra)),
            out_specs=vmem,
            scratch_shapes=key_scratch,
            name="lookup",
            compiler_params=params(),
        )(chunk, grad, *extra)

    order = list(range(groups - 1, 0, -1))
    if groups == 8:
        order = [7, 1, 6, 2, 3, 4, 5]
    early = [lookup(arrived[step], []) for step in order[:EARLY]]
    *shares, early = lax.optimization_barrier((*shares, early))
    tail, *early = pl.pallas_call(
        functools.partial(tail_kernel, slabs, len(early)),
        out_shape=[jax.ShapeDtypeStruct((2 * SUPER, LANES), BF16)]
        + [jax.ShapeDtypeStruct((back_rows, LANES), BF16)] * len(early),
        in_specs=[smem] + [vmem] * (1 + slabs) + [pl.BlockSpec(memory_space=pl.ANY)] * len(early),
        out_specs=[vmem] + [pl.BlockSpec(memory_space=pl.ANY)] * len(early),
        scratch_shapes=[
            pltpu.VMEM((slabs, SUPER, across), F32),
            pltpu.SemaphoreType.DMA((len(early),)),
        ],
        input_output_aliases={2 + slabs + number: 1 + number for number in range(len(early))},
        name="tail",
        compiler_params=params(),
    )(slab_one, margins, *shares, *early)

    returned = [None] * groups
    for step, answer in zip(order, early):
        returned[step] = send_back(answer, step)
    for step in order[EARLY:]:
        returned[step] = send_back(lookup(arrived[step], [tail]), step)
    returned[0] = lookup(arrived[0], [])

    trade_grad, margin, expected = pl.pallas_call(
        functools.partial(unpack_kernel, groups, width, padded, path_count * slabs),
        out_shape=[
            jax.ShapeDtypeStruct((capacity, path_count), BF16),
            jax.ShapeDtypeStruct((nets, path_count), F32),
            jax.ShapeDtypeStruct((nets,), F32),
        ],
        in_specs=[smem, smem, vmem] + [vmem] * (groups + 1),
        out_specs=[vmem, vmem, smem],
        scratch_shapes=[pltpu.VMEM((groups, back_rows, LANES), BF16)],
        name="unpack",
        compiler_params=params(),
    )(me_one, counts, weight, *returned, tail)
    return (margin, expected, trade_grad)


def solution(mesh):
    placed = (
        P("trade", "path"),
        P("trade"),
        P("trade"),
        P(),
        P(),
        P("trade"),
        P(),
        P("path"),
        P(None, "path"),
    )
    return jax.shard_map(
        shards,
        mesh=mesh,
        in_specs=placed,
        out_specs=(P(None, "path"), P(), P("trade", "path")),
        check_vma=False,
    )
```
